256 devices in a mesh: lev: 64 (over z, x, core), col: 4 (over y).
Axes of the slice: x: 4, y: 4, z: 8, core: 2. Of those that a mesh axis runs over, the one named last changes fastest.
Arguments:
- probe_field: bfloat16 [128, 16, 4, 16384], P('lev', None, 'col'), may hold values from -6 to 6
- vertical_corr: bfloat16 [128, 128], replicated, may hold values from -0.5 to 0.5
- kernel_tiles: bfloat16 [4, 128, 9, 128, 128], P('col', 'lev'), may hold values from -0.1875 to 0.1875
- column_tile: int32 [4, 128, 9], P('col', 'lev'), may hold values from 0 to 511, as said below
- tile_counts: int32 [4, 128], P('col', 'lev'), may hold values from 1 to 9, as said below
Outputs:
- sketch: bfloat16 [128, 16, 4, 16384], P('lev', None, 'col')
The draws below stay inside these ranges and needn't reach their ends.
Inputs may be any that keep to these rules, and one draw needn't show every extreme that they name: For k < tile_counts[j, q], column_tile[j, q, k] is the tile of band j + a at position (q + b) modulo 128, with a and b in -1, 0, 1 and band j + a within the bands; the used entries of one row tile are distinct, entry 0 is the row tile itself (j * 128 + q), and unused slots hold the row tile itself. `tile_counts`: row tiles of bands 1 and 2 use all 9 slots.
All inputs are finite; a program needn't handle non-finite values.
Results may differ from the reference program's by a relative error of at most 0.0049.
Values may be sent and summed in bfloat16 or wider, within the bound.
A program may use at most 64 MiB of HBM per device.

```python
import jax
import jax.numpy as jnp
from jax import lax

PROBES = 16
TILE = 128
KMAX = 9
L = 128
TD = 128
BANDS = 4


def neighbor_layout(key):
    base_key = jax.random.fold_in(key, 11)
    key_scores, key_counts = jax.random.split(base_key)
    band_ids = jnp.arange(BANDS, dtype=jnp.int32)[:, None]
    position_ids = jnp.arange(TD, dtype=jnp.int32)[None, :]
    band_steps = jnp.array([-1, -1, -1, 0, 0, 1, 1, 1], jnp.int32)
    position_steps = jnp.array([-1, 0, 1, -1, 1, -1, 0, 1], jnp.int32)
    target_band = jnp.broadcast_to(band_ids[:, :, None] + band_steps, (BANDS, TD, 8))
    allowed = (target_band >= 0) & (target_band < BANDS)
    scores = jax.random.randint(key_scores, (BANDS, TD, 8), 0, 1 << 20) * 8 + jnp.arange(8, dtype=jnp.int32)
    ranked = jnp.where(allowed, scores + (1 << 24), scores)
    ordering = jnp.argsort(-ranked, axis=-1, stable=True)
    chosen_band = jnp.take_along_axis(target_band, ordering, axis=-1)
    chosen_position = (position_ids[:, :, None] + jnp.take(position_steps, ordering)) % TD
    chosen = chosen_band * TD + chosen_position
    self_index = band_ids * TD + position_ids
    allowed_count = 1 + jnp.sum(allowed.astype(jnp.int32), axis=-1)
    raw_counts = jax.random.randint(key_counts, (BANDS, TD), 0, 1 << 20)
    row_counts = 1 + raw_counts % allowed_count
    forced = (band_ids == 1) | (band_ids == BANDS - 2)
    row_counts = jnp.where(forced, KMAX, row_counts)
    full_rows = jnp.concatenate([self_index[:, :, None] + jnp.zeros((BANDS, TD, 1), jnp.int32), chosen], axis=-1)
    slot_ids = jnp.arange(KMAX, dtype=jnp.int32)[None, None, :]
    column_tile = jnp.where(slot_ids < row_counts[:, :, None], full_rows, self_index[:, :, None])
    return (column_tile.astype(jnp.int32), row_counts.astype(jnp.int32))


def draw_column_tile(key, part):
    return neighbor_layout(key)[0]


def draw_tile_counts(key, part):
    return neighbor_layout(key)[1]


def shard_levels(own_key, shape, pieces, low, top_value):
    gain = 1.0
    for dim, parts in pieces:
        heights = jax.random.uniform(jax.random.fold_in(jax.random.fold_in(own_key, 6), dim), (parts,), jnp.float32, low / len(pieces), top_value / len(pieces))
        gain = gain * jnp.repeat(jnp.exp(heights), shape[dim] // parts).reshape((-1,) + (1,) * (len(shape) - 1 - dim))
    return gain


def scatter_about(own_key, shape, width, most, cuts=(), kind=jnp.bfloat16):
    values = jax.random.normal(own_key, shape, jnp.float32) * width
    if len(cuts) > 0:
        values = shard_levels(own_key, shape, cuts, -0.22, 0.18) * values
    return jnp.clip(values, min=-most, max=most).astype(kind)


def setup_inputs(seed: int = 0) -> dict:
    key_list = jax.random.split(jax.random.key(seed), 6)
    probe_field = scatter_about(key_list[0], (L, PROBES, BANDS, TD * TILE), 1.0, 6.0, ((0, 64), (2, 4)))
    vertical_corr = scatter_about(key_list[1], (L, L), L ** -0.5, 0.5)
    kernel_tiles = scatter_about(key_list[2], (BANDS, TD, KMAX, TILE, TILE), (TILE * KMAX) ** -0.5, 0.1875, ((0, 4), (1, 64)))
    column_tile = draw_column_tile(jax.random.fold_in(key_list[5], 71), 0)
    tile_counts = draw_tile_counts(jax.random.fold_in(key_list[5], 71), 0)
    return dict(probe_field=probe_field, vertical_corr=vertical_corr, kernel_tiles=kernel_tiles, column_tile=column_tile, tile_counts=tile_counts)


def reference(probe_field, vertical_corr, kernel_tiles, column_tile, tile_counts):
    flattened = probe_field.reshape(L * PROBES, BANDS * TD, TILE)
    live_mask = jnp.arange(KMAX, dtype=jnp.int32)[None, None, :] < tile_counts[:, :, None]

    def one_band(items):
        band_tiles, band_columns, band_live = items
        slot_weights = band_tiles.astype(jnp.float32) * band_live[:, :, None, None].astype(jnp.float32)
        picked = jnp.take(flattened, band_columns.reshape(-1).astype(jnp.int32), axis=1)
        picked = picked.reshape(L * PROBES, TD, KMAX, TILE).astype(jnp.float32)
        mixed_tiles = jnp.einsum("rtki,tkoi->rto", picked, slot_weights)
        return mixed_tiles.astype(jnp.bfloat16)

    bands_out = lax.map(one_band, (kernel_tiles, column_tile, live_mask))
    horizontal = jnp.transpose(bands_out, (1, 0, 2, 3)).reshape(L, PROBES * BANDS * TD * TILE)
    sketch = jnp.dot(vertical_corr, horizontal, preferred_element_type=jnp.float32)
    return sketch.astype(jnp.bfloat16).reshape(L, PROBES, BANDS, TD * TILE)
```

```python
import functools

import jax
import jax.numpy as jnp
from jax import lax
from jax.experimental import pallas as pl
from jax.experimental.pallas import tpu as pltpu
from jax.sharding import PartitionSpec as P

MESH = pl.DeviceIdType.MESH
NZ = 8
NE = 8
NL = NZ * NE
TS = 128
LAG_EDGE = 2
LAG_SUM = 3


def offset(k):
    odd = lax.rem(k, 2)
    return odd * lax.div(k + 1, 2) - (1 - odd) * lax.div(k, 2)


def kernel(
    x_ref, v_ref, tiles_ref, slot_ref, count_ref, out_ref,
    field, weights, weights_in, kron, tiles, vert,
    own, part_out, part_in, mixed, result,
    sync, local_sem, x_send, x_recv, w_send, w_recv,
    e_send, e_recv, p_send, p_recv, b_send, b_recv,
):
    me = lax.axis_index("lev")
    band = lax.axis_index("col")
    z = lax.div(me, NE)
    e = lax.rem(me, NE)
    up = lax.rem(band + 1, 4)
    down = lax.rem(band + 3, 4)
    right = lax.rem(me + 1, NL)
    left = lax.rem(me + NL - 1, NL)

    tiles_copy = pltpu.make_async_copy(tiles_ref, tiles, local_sem.at[0])
    vert_copy = pltpu.make_async_copy(v_ref, vert, local_sem.at[1])
    tiles_copy.start()
    vert_copy.start()

    barrier = pltpu.get_barrier_semaphore()
    for i in range(1, NE):
        pl.semaphore_signal(
            barrier, inc=1, device_id={"lev": z * NE + lax.rem(e + i, NE)}, device_id_type=MESH
        )
    for i in range(1, NZ):
        pl.semaphore_signal(
            barrier, inc=1, device_id={"lev": lax.rem(z + i, NZ) * NE + e}, device_id_type=MESH
        )
    pl.semaphore_signal(barrier, inc=1, device_id={"col": up}, device_id_type=MESH)
    pl.semaphore_signal(barrier, inc=1, device_id={"col": down}, device_id_type=MESH)
    pl.semaphore_wait(barrier, NE + NZ)
    for i in range(1, NZ):
        pl.semaphore_signal(
            sync, inc=1, device_id={"lev": lax.rem(z + i, NZ) * NE + e}, device_id_type=MESH
        )
    pl.semaphore_wait(sync, NZ - 1)

    def columns(owner):
        return pl.ds(pl.multiple_of(owner * 256, 256), 256)

    def send_block(i, carry):
        there = lax.rem(z + offset(lax.div(i, NE)) + NZ, NZ)
        to = there * NE + lax.rem(e + lax.rem(i, NE), NE)
        pltpu.make_async_remote_copy(
            src_ref=x_ref.at[:, :, columns(to)],
            dst_ref=field.at[me, :, :, pl.ds(TS, 2 * TS)],
            send_sem=x_send,
            recv_sem=x_recv.at[z],
            device_id={"lev": to},
            device_id_type=MESH,
        ).start()
        return carry

    pltpu.make_async_copy(
        x_ref.at[:, :, columns(me)], field.at[me, :, :, pl.ds(TS, 2 * TS)], x_recv.at[z]
    ).start()
    lax.fori_loop(1, NL, send_block, 0)

    tiles_copy.wait()
    weights[...] = jnp.zeros_like(weights)
    for t in range(2):
        place = []
        for k in range(9):
            slot = slot_ref[t, k]
            step = lax.div(slot, 128) - band + 1
            shift = lax.rem(lax.rem(slot, 128) - (me * 2 + t) + 129 + 128, 128)
            live = count_ref[0, t] > k
            place.append(jnp.where(live, step * 3 + shift, -1))
        for a in range(3):
            for b in range(3):
                block = jnp.zeros((TS, TS), jnp.float32)
                for k in range(9):
                    hit = jnp.where(place[k] == a * 3 + b, 1.0, 0.0).astype(jnp.float32)
                    block = block + hit * tiles[t, k].astype(jnp.float32)
                weights[a, t * TS:(t + 1) * TS, (t + b) * TS:(t + b + 1) * TS] = block.astype(
                    jnp.bfloat16
                )
    w_up = pltpu.make_async_remote_copy(
        src_ref=weights.at[2], dst_ref=weights_in.at[0], send_sem=w_send.at[0],
        recv_sem=w_recv.at[0], device_id={"col": up}, device_id_type=MESH,
    )
    w_down = pltpu.make_async_remote_copy(
        src_ref=weights.at[0], dst_ref=weights_in.at[1], send_sem=w_send.at[1],
        recv_sem=w_recv.at[1], device_id={"col": down}, device_id_type=MESH,
    )
    w_up.start()
    w_down.start()

    vert_copy.wait()
    spread = (
        lax.div(lax.broadcasted_iota(jnp.int32, (TS, 1024), 1), 8)
        == lax.broadcasted_iota(jnp.int32, (TS, 1024), 0)
    ).astype(jnp.bfloat16)

    def kron_rows(c, carry):
        rows = (
            c * 16 + lax.div(lax.broadcasted_iota(jnp.int32, (TS, TS), 0), 8)
            == lax.broadcasted_iota(jnp.int32, (TS, TS), 1)
        ).astype(jnp.bfloat16)
        picked = jnp.dot(rows, vert[...], preferred_element_type=jnp.float32).astype(jnp.bfloat16)
        wide = jnp.dot(picked, spread, preferred_element_type=jnp.float32)
        same = lax.rem(lax.broadcasted_iota(jnp.int32, (TS, 1024), 0), 8) == lax.rem(
            lax.broadcasted_iota(jnp.int32, (TS, 1024), 1), 8
        )
        kron[pl.ds(pl.multiple_of(c * TS, TS), TS), :] = jnp.where(same, wide, 0.0).astype(
            jnp.bfloat16
        )
        return carry

    lax.fori_loop(0, 8, kron_rows, 0)

    w_up.wait()
    w_down.wait()

    def group(k):
        return lax.rem(z - offset(k) + NZ, NZ)

    def edge(g, side):
        source = field.at[pl.ds(g * NE, NE), :, :, pl.ds(TS if side == 0 else 2 * TS, TS)]
        target = field.at[pl.ds(g * NE, NE), :, :, pl.ds(3 * TS if side == 0 else 0, TS)]
        return pltpu.make_async_remote_copy(
            src_ref=source, dst_ref=target, send_sem=e_send.at[g, side],
            recv_sem=e_recv.at[g, side], device_id={"lev": left if side == 0 else right},
            device_id_type=MESH,
        )

    def part(g, side):
        return pltpu.make_async_remote_copy(
            src_ref=part_out.at[side, g], dst_ref=part_in.at[side, g],
            send_sem=p_send.at[g, side], recv_sem=p_recv.at[g, side],
            device_id={"col": down if side == 0 else up}, device_id_type=MESH,
        )

    nt = (((1,), (1,)), ((), ()))

    def step(k, carry):
        @pl.when(k < NZ)
        def _():
            g = group(k)
            arrived = field.at[pl.ds(g * NE, NE), :, :, pl.ds(TS, 2 * TS)]
            pltpu.make_async_copy(arrived, arrived, x_recv.at[g]).wait()
            edge(g, 0).start()
            edge(g, 1).start()

        @pl.when((k >= LAG_EDGE) & (k < NZ + LAG_EDGE))
        def _():
            g = group(k - LAG_EDGE)
            edge(g, 0).wait()
            edge(g, 1).wait()
            rows = field[pl.ds(g * NE, NE)].reshape(256, 4 * TS)
            for side in range(2):
                part_out[side, g] = lax.dot_general(
                    rows, weights_in[side], nt, preferred_element_type=jnp.float32
                ).astype(jnp.bfloat16)
                part(g, side).start()
            own[g] = lax.dot_general(rows, weights[1], nt, preferred_element_type=jnp.float32)

        @pl.when(k >= LAG_SUM)
        def _():
            g = group(k - LAG_SUM)
            part(g, 0).wait()
            part(g, 1).wait()
            total = own[g] + part_in[0, g].astype(jnp.float32) + part_in[1, g].astype(jnp.float32)
            total = total.reshape(16, 2, 8, 256)
            at = pl.ds(pl.multiple_of(g * TS, TS), TS)
            for half in range(2):
                mixed[half, at, :] = total[:, half].reshape(TS, 256).astype(jnp.bfloat16)

        return carry

    lax.fori_loop(0, NZ + LAG_SUM, step, 0)

    def answer(m, carry):
        there = lax.rem(z + offset(NZ - 1 - m) + NZ, NZ)
        rows = kron[pl.ds(pl.multiple_of(there * TS, TS), TS), :]
        halves = [
            jnp.dot(rows, mixed[half], preferred_element_type=jnp.float32).reshape(16, 1, 8, 256)
            for half in range(2)
        ]
        both = jnp.concatenate(halves, axis=1).reshape(NE, 2, 16, 256)
        result[pl.ds(there * NE, NE)] = both.astype(jnp.bfloat16)

        def send_back(i, inner):
            to = there * NE + lax.rem(e + i, NE)

            @pl.when(to != me)
            def _():
                pltpu.make_async_remote_copy(
                    src_ref=result.at[to], dst_ref=out_ref.at[:, :, columns(me)],
                    send_sem=b_send, recv_sem=b_recv, device_id={"lev": to}, device_id_type=MESH,
                ).start()

            @pl.when(to == me)
            def _():
                pltpu.make_async_copy(result.at[me], out_ref.at[:, :, columns(me)], b_recv).start()

            return inner

        lax.fori_loop(0, NE, send_back, 0)
        return carry

    lax.fori_loop(0, NZ, answer, 0)

    others = field.at[pl.ds(0, NL - 1), :, :, pl.ds(TS, 2 * TS)]
    pltpu.make_async_copy(others, others, x_send).wait()
    others = result.at[pl.ds(0, NL - 1)]
    pltpu.make_async_copy(others, others, b_send).wait()
    pltpu.make_async_copy(out_ref, out_ref, b_recv).wait()


def body(probe_field, vertical_corr, kernel_tiles, column_tile, tile_counts):
    bf16 = jnp.bfloat16
    dma = pltpu.SemaphoreType.DMA
    any_space = pl.BlockSpec(memory_space=pl.ANY)
    smem = pl.BlockSpec(memory_space=pltpu.SMEM)
    out = pl.pallas_call(
        kernel,
        out_shape=jax.ShapeDtypeStruct((2, 16, NL * 256), bf16),
        in_specs=[any_space, any_space, any_space, smem, smem],
        out_specs=any_space,
        scratch_shapes=[
            pltpu.VMEM((NL, 2, 16, 4 * TS), bf16),
            pltpu.VMEM((3, 256, 512), bf16),
            pltpu.VMEM((2, 256, 512), bf16),
            pltpu.VMEM((1024, 1024), bf16),
            pltpu.VMEM((2, 9, TS, TS), bf16),
            pltpu.VMEM((TS, TS), bf16),
            pltpu.VMEM((NZ, 256, 256), jnp.float32),
            pltpu.VMEM((2, NZ, 256, 256), bf16),
            pltpu.VMEM((2, NZ, 256, 256), bf16),
            pltpu.VMEM((2, 1024, 256), bf16),
            pltpu.VMEM((NL, 2, 16, 256), bf16),
            pltpu.SemaphoreType.REGULAR,
            dma((2,)),
            dma,
            dma((NZ,)),
            dma((2,)),
            dma((2,)),
            dma((NZ, 2)),
            dma((NZ, 2)),
            dma((NZ, 2)),
            dma((NZ, 2)),
            dma,
            dma,
        ],
        compiler_params=pltpu.CompilerParams(
            collective_id=0, has_side_effects=True, vmem_limit_bytes=40 * 1024 * 1024
        ),
    )(
        probe_field.reshape(2, 16, NL * 256),
        vertical_corr,
        kernel_tiles.reshape(2, 9, TS, TS),
        column_tile.reshape(2, 9),
        tile_counts,
    )
    return out.reshape(2, 16, 1, NL * 256)


def solution(mesh):
    placed = (
        P("lev", None, "col", None),
        P(),
        P("col", "lev", None, None, None),
        P("col", "lev", None),
        P("col", "lev"),
    )
    return jax.shard_map(
        body, mesh=mesh, in_specs=placed, out_specs=P("lev", None, "col", None), check_vma=False
    )
```

```python
import jax
import jax.numpy as jnp
from jax import lax
from jax.experimental import pallas as pl
from jax.experimental.pallas import tpu as pltpu
from jax.sharding import PartitionSpec as P

MESH = pl.DeviceIdType.MESH
NZ = 8
NX = 4
NE = 2 * NX
NL = NZ * NE
TS = 128
ROUNDS = 2 * NX
WINDOW = 3
LAG_EDGE = 2
LAG_SUM = 3


def offset(k):
    odd = lax.rem(k, 2)
    return odd * lax.div(k + 1, 2) - (1 - odd) * lax.div(k, 2)


def kernel(
    x_ref, v_ref, tiles_ref, slot_hbm, count_hbm, out_ref,
    field, weights, weights_in, kron, tiles, vert, slot_ref, count_ref,
    own, part_out, part_in, mixed, result,
    local_sem, x_send, x_recv, w_send, w_recv,
    e_send, e_recv, p_send, p_recv, b_send, b_recv,
):
    me = lax.axis_index("lev")
    band = lax.axis_index("col")
    z = lax.div(me, NE)
    e = lax.rem(me, NE)
    x = lax.div(e, 2)
    core = lax.rem(e, 2)
    up = lax.rem(band + 1, 4)
    down = lax.rem(band + 3, 4)
    right = lax.rem(me + 1, NL)
    left = lax.rem(me + NL - 1, NL)

    barrier = pltpu.get_barrier_semaphore()

    def greet(i, carry):
        pl.semaphore_signal(
            barrier, inc=1, device_id={"lev": lax.rem(me + i, NL)}, device_id_type=MESH
        )
        return carry

    pl.semaphore_signal(barrier, inc=1, device_id={"col": up}, device_id_type=MESH)
    pl.semaphore_signal(barrier, inc=1, device_id={"col": down}, device_id_type=MESH)
    lax.fori_loop(1, NL, greet, 0)

    local = [
        pltpu.make_async_copy(source, target, local_sem.at[i])
        for i, (source, target) in enumerate(
            [(slot_hbm, slot_ref), (count_hbm, count_ref), (tiles_ref, tiles), (v_ref, vert)]
        )
    ]
    for copy in local:
        copy.start()

    pl.semaphore_wait(barrier, NL + 1)

    def columns(owner):
        return pl.ds(pl.multiple_of(owner * 256, 256), 256)

    def send_block(k, i):
        half = lax.div(k, NX)
        there = lax.rem(z + offset(lax.div(i, 2)) + NZ, NZ)
        place = lax.rem(x + lax.rem(k, NX), NX) * 2 + lax.rem(core + lax.rem(i, 2), 2)
        to = there * NE + place
        pltpu.make_async_remote_copy(
            src_ref=x_ref.at[:, half, :, columns(to)],
            dst_ref=field.at[half, z, e, :, :, pl.ds(TS, 2 * TS)],
            send_sem=x_send.at[k],
            recv_sem=x_recv.at[half, x],
            device_id={"lev": to},
            device_id_type=MESH,
        ).start()

    def keep_block(half):
        pltpu.make_async_copy(
            x_ref.at[:, half, :, columns(me)],
            field.at[half, z, e, :, :, pl.ds(TS, 2 * TS)],
            x_recv.at[half, x],
        ).start()

    def send_round(k, first=0):
        def one(i, carry):
            send_block(k, i)
            return carry

        lax.fori_loop(first, 2 * NZ, one, 0)

    send_round(0, 1)
    keep_block(0)
    keep_block(1)
    for k in range(1, WINDOW):
        send_round(k)

    for copy in local[:3]:
        copy.wait()
    nothing = jnp.zeros((TS, TS), jnp.bfloat16)
    for t in range(2):
        unused = pl.ds((1 - t) * 3 * TS, TS)
        for side in range(2):
            weights_in[side, t * TS:(t + 1) * TS, unused] = nothing
        weights[1, t * TS:(t + 1) * TS, unused] = nothing
        place = []
        for k in range(9):
            slot = slot_ref[t, k]
            step = lax.div(slot, 128) - band + 1
            shift = lax.rem(lax.rem(slot, 128) - (me * 2 + t) + 129 + 128, 128)
            live = count_ref[0, t] > k
            place.append(jnp.where(live, step * 3 + shift, -1))
        for a in range(3):
            for b in range(3):
                block = jnp.zeros((TS, TS), jnp.float32)
                for k in range(9):
                    hit = jnp.where(place[k] == a * 3 + b, 1.0, 0.0).astype(jnp.float32)
                    block = block + hit * tiles[t, k].astype(jnp.float32)
                weights[a, t * TS:(t + 1) * TS, (t + b) * TS:(t + b + 1) * TS] = block.astype(
                    jnp.bfloat16
                )
    matrices = []
    for side in range(2):
        for t in range(2):
            at = (pl.ds(t * TS, TS), pl.ds(t * TS, 3 * TS))
            matrices.append(
                pltpu.make_async_remote_copy(
                    src_ref=weights.at[(2 - 2 * side, *at)],
                    dst_ref=weights_in.at[(side, *at)],
                    send_sem=w_send.at[side, t],
                    recv_sem=w_recv.at[side, t],
                    device_id={"col": down if side else up},
                    device_id_type=MESH,
                )
            )
    for copy in matrices:
        copy.start()

    local[3].wait()
    spread = (
        lax.div(lax.broadcasted_iota(jnp.int32, (TS, 1024), 1), 8)
        == lax.broadcasted_iota(jnp.int32, (TS, 1024), 0)
    ).astype(jnp.bfloat16)

    def kron_rows(c, carry):
        rows = (
            c * 16 + lax.div(lax.broadcasted_iota(jnp.int32, (TS, TS), 0), 8)
            == lax.broadcasted_iota(jnp.int32, (TS, TS), 1)
        ).astype(jnp.bfloat16)
        picked = jnp.dot(rows, vert[...], preferred_element_type=jnp.float32).astype(jnp.bfloat16)
        wide = jnp.dot(picked, spread, preferred_element_type=jnp.float32)
        same = lax.rem(lax.broadcasted_iota(jnp.int32, (TS, 1024), 0), 8) == lax.rem(
            lax.broadcasted_iota(jnp.int32, (TS, 1024), 1), 8
        )
        kron[c] = jnp.where(same, wide, 0.0).reshape(NX, 32, 1024).astype(jnp.bfloat16)
        return carry

    lax.fori_loop(0, 8, kron_rows, 0)

    def group(r):
        return lax.rem(x - r + NX, NX)

    def edge(half, g, side):
        rows = (half, slice(None), pl.ds(g * 2, 2), slice(None), slice(None))
        return pltpu.make_async_remote_copy(
            src_ref=field.at[(*rows, pl.ds(TS if side == 0 else 2 * TS, TS))],
            dst_ref=field.at[(*rows, pl.ds(3 * TS if side == 0 else 0, TS))],
            send_sem=e_send.at[half, g, side],
            recv_sem=e_recv.at[half, g, side],
            device_id={"lev": left if side == 0 else right},
            device_id_type=MESH,
        )

    def part(half, g, side):
        return pltpu.make_async_remote_copy(
            src_ref=part_out.at[side, half, g],
            dst_ref=part_in.at[side, half, g],
            send_sem=p_send.at[half, g, side],
            recv_sem=p_recv.at[half, g, side],
            device_id={"col": down if side == 0 else up},
            device_id_type=MESH,
        )

    nt = (((1,), (1,)), ((), ()))

    def answer(half):
        def one_round(r, carry):
            place = lax.rem(x + r, NX)
            rows = kron[:, place].reshape(256, 1024)
            block = jnp.dot(
                rows, mixed[half].reshape(1024, 256), preferred_element_type=jnp.float32
            )
            result[half, :, pl.ds(place * 2, 2)] = block.reshape(NZ, 2, 2, 8, 256).astype(
                jnp.bfloat16
            )

            def send_back(i, inner):
                there = lax.rem(z + offset(lax.div(i, 2)) + NZ, NZ)
                spot = place * 2 + lax.rem(core + lax.rem(i, 2), 2)
                to = there * NE + spot

                @pl.when(to != me)
                def _():
                    pltpu.make_async_remote_copy(
                        src_ref=result.at[half, there, spot],
                        dst_ref=out_ref.at[:, half, :, columns(me)],
                        send_sem=b_send,
                        recv_sem=b_recv,
                        device_id={"lev": to},
                        device_id_type=MESH,
                    ).start()

                @pl.when(to == me)
                def _():
                    pltpu.make_async_copy(
                        result.at[half, z, e], out_ref.at[:, half, :, columns(me)], b_recv
                    ).start()

                return inner

            lax.fori_loop(0, 2 * NZ, send_back, 0)
            return carry

        lax.fori_loop(0, NX, one_round, 0)

    def step(k, carry):
        @pl.when(k < ROUNDS)
        def _():
            half = lax.div(k, NX)
            g = group(lax.rem(k, NX))
            arrived = field.at[half, :, pl.ds(g * 2, 2), :, :, pl.ds(TS, 2 * TS)]
            pltpu.make_async_copy(arrived, arrived, x_recv.at[half, g]).wait()
            edge(half, g, 0).start()
            edge(half, g, 1).start()

        @pl.when(k < ROUNDS - WINDOW)
        def _():
            later = k + WINDOW
            send_round(later, jnp.where(later == NX, 1, 0))

        @pl.when(k == LAG_EDGE)
        def _():
            for copy in matrices:
                copy.wait()

        @pl.when((k >= LAG_EDGE) & (k < ROUNDS + LAG_EDGE))
        def _():
            now = k - LAG_EDGE
            half = lax.div(now, NX)
            g = group(lax.rem(now + 1, NX))
            edge(half, g, 0).wait()
            edge(half, g, 1).wait()
            rows = field[half, :, pl.ds(g * 2, 2)].reshape(256, 4 * TS)
            for side in range(2):
                part_out[side, half, g] = lax.dot_general(
                    rows, weights_in[side], nt, preferred_element_type=jnp.float32
                ).astype(jnp.bfloat16)
                part(half, g, side).start()
            own[half, g] = lax.dot_general(
                rows, weights[1], nt, preferred_element_type=jnp.float32
            )

        @pl.when(k >= LAG_SUM)
        def _():
            now = k - LAG_SUM
            half = lax.div(now, NX)
            g = group(lax.rem(now + 1, NX))
            part(half, g, 0).wait()
            part(half, g, 1).wait()
            total = (
                own[half, g]
                + part_in[0, half, g].astype(jnp.float32)
                + part_in[1, half, g].astype(jnp.float32)
            )
            mixed[half, :, g] = total.reshape(NZ, 32, 256).astype(jnp.bfloat16)

            @pl.when(lax.rem(now, NX) == NX - 1)
            def _():
                answer(half)

        return carry

    lax.fori_loop(0, ROUNDS + LAG_SUM, step, 0)

    for k in range(ROUNDS):
        if k % NX == 0:
            for rows in ((pl.ds(0, NZ - 1), pl.ds(0, 2)), (NZ - 1, pl.ds(0, 1))):
                block = field.at[(0, *rows, slice(None), slice(None), pl.ds(TS, 2 * TS))]
                pltpu.make_async_copy(block, block, x_send.at[k]).wait()
        else:
            block = field.at[0, :, pl.ds(0, 2), :, :, pl.ds(TS, 2 * TS)]
            pltpu.make_async_copy(block, block, x_send.at[k]).wait()
    block = out_ref.at[:, :, :, pl.ds(0, (NL - 1) * 256)]
    pltpu.make_async_copy(block, block, b_send).wait()
    pltpu.make_async_copy(out_ref, out_ref, b_recv).wait()


def body(probe_field, vertical_corr, kernel_tiles, column_tile, tile_counts):
    bf16 = jnp.bfloat16
    dma = pltpu.SemaphoreType.DMA
    any_space = pl.BlockSpec(memory_space=pl.ANY)
    operands = [
        probe_field.reshape(2, 2, 8, NL * 256),
        vertical_corr,
        kernel_tiles.reshape(2, 9, TS, TS),
        column_tile.reshape(2, 9),
        tile_counts,
    ]
    operands = [pltpu.with_memory_space_constraint(a, pltpu.HBM) for a in operands]
    out = pl.pallas_call(
        kernel,
        out_shape=jax.ShapeDtypeStruct((2, 2, 8, NL * 256), bf16),
        in_specs=[any_space] * 5,
        out_specs=any_space,
        scratch_shapes=[
            pltpu.VMEM((2, NZ, NE, 2, 8, 4 * TS), bf16),
            pltpu.VMEM((3, 256, 512), bf16),
            pltpu.VMEM((2, 256, 512), bf16),
            pltpu.VMEM((NZ, NX, 32, 1024), bf16),
            pltpu.VMEM((2, 9, TS, TS), bf16),
            pltpu.VMEM((TS, TS), bf16),
            pltpu.SMEM((2, 9), jnp.int32),
            pltpu.SMEM((1, 2), jnp.int32),
            pltpu.VMEM((2, NX, 256, 256), jnp.float32),
            pltpu.VMEM((2, 2, NX, 256, 256), bf16),
            pltpu.VMEM((2, 2, NX, 256, 256), bf16),
            pltpu.VMEM((2, NZ, NX, 32, 256), bf16),
            pltpu.VMEM((2, NZ, NE, 2, 8, 256), bf16),
            dma((4,)),
            dma((ROUNDS,)),
            dma((2, NX)),
            dma((2, 2)),
            dma((2, 2)),
            dma((2, NX, 2)),
            dma((2, NX, 2)),
            dma((2, NX, 2)),
            dma((2, NX, 2)),
            dma,
            dma,
        ],
        compiler_params=pltpu.CompilerParams(
            collective_id=0, has_side_effects=True, vmem_limit_bytes=40 * 1024 * 1024
        ),
    )(*operands)
    return out.reshape(2, 16, 1, NL * 256)


def solution(mesh):
    placed = (
        P("lev", None, "col", None),
        P(),
        P("col", "lev", None, None, None),
        P("col", "lev", None),
        P("col", "lev"),
    )
    return jax.shard_map(
        body, mesh=mesh, in_specs=placed, out_specs=P("lev", None, "col", None), check_vma=False
    )
```

```python
import jax
import jax.numpy as jnp
from jax import lax
from jax.experimental import pallas as pl
from jax.experimental.pallas import tpu as pltpu
from jax.sharding import PartitionSpec as P

MESH = pl.DeviceIdType.MESH
NZ = 8
NX = 4
NE = 2 * NX
NL = NZ * NE
TS = 128
ROUNDS = 2 * NX
WINDOW = 3
LAG_EDGE = 2
LAG_SUM = 4


def offset(k):
    odd = lax.rem(k, 2)
    return odd * lax.div(k + 1, 2) - (1 - odd) * lax.div(k, 2)


def kernel(
    x_ref, v_ref, tiles_ref, slot_hbm, count_hbm, out_ref,
    field, weights, weights_in, kron, tiles, vert, slot_ref, count_ref,
    own, part_out, part_in, mixed, result,
    local_sem, x_send, x_recv, w_send, w_recv,
    e_send, e_recv, p_send, p_recv, b_send, b_recv,
):
    me = lax.axis_index("lev")
    band = lax.axis_index("col")
    z = lax.div(me, NE)
    e = lax.rem(me, NE)
    x = lax.div(e, 2)
    core = lax.rem(e, 2)
    up = lax.rem(band + 1, 4)
    down = lax.rem(band + 3, 4)
    right = lax.rem(me + 1, NL)
    left = lax.rem(me + NL - 1, NL)

    barrier = pltpu.get_barrier_semaphore()

    def greet(i, carry):
        pl.semaphore_signal(
            barrier, inc=1, device_id={"lev": lax.rem(me + i, NL)}, device_id_type=MESH
        )
        return carry

    pl.semaphore_signal(barrier, inc=1, device_id={"col": up}, device_id_type=MESH)
    pl.semaphore_signal(barrier, inc=1, device_id={"col": down}, device_id_type=MESH)
    lax.fori_loop(1, NL, greet, 0)

    local = [
        pltpu.make_async_copy(source, target, local_sem.at[i])
        for i, (source, target) in enumerate(
            [(slot_hbm, slot_ref), (count_hbm, count_ref), (tiles_ref, tiles), (v_ref, vert)]
        )
    ]
    for copy in local:
        copy.start()

    for copy in local[:3]:
        copy.wait()
    nothing = jnp.zeros((TS, TS), jnp.bfloat16)
    for t in range(2):
        unused = pl.ds((1 - t) * 3 * TS, TS)
        for side in range(2):
            weights_in[side, t * TS:(t + 1) * TS, unused] = nothing
        weights[1, t * TS:(t + 1) * TS, unused] = nothing
        place = []
        for k in range(9):
            slot = slot_ref[t, k]
            step = lax.div(slot, 128) - band + 1
            shift = lax.rem(lax.rem(slot, 128) - (me * 2 + t) + 129 + 128, 128)
            live = count_ref[0, t] > k
            place.append(jnp.where(live, step * 3 + shift, -1))
        for a in range(3):
            for b in range(3):
                block = jnp.zeros((TS, TS), jnp.float32)
                for k in range(9):
                    hit = jnp.where(place[k] == a * 3 + b, 1.0, 0.0).astype(jnp.float32)
                    block = block + hit * tiles[t, k].astype(jnp.float32)
                weights[a, t * TS:(t + 1) * TS, (t + b) * TS:(t + b + 1) * TS] = block.astype(
                    jnp.bfloat16
                )
    matrices = []
    for side in range(2):
        for t in range(2):
            at = (pl.ds(t * TS, TS), pl.ds(t * TS, 3 * TS))
            matrices.append(
                pltpu.make_async_remote_copy(
                    src_ref=weights.at[(2 - 2 * side, *at)],
                    dst_ref=weights_in.at[(side, *at)],
                    send_sem=w_send.at[side, t],
                    recv_sem=w_recv.at[side, t],
                    device_id={"col": down if side else up},
                    device_id_type=MESH,
                )
            )

    pl.semaphore_wait(barrier, NL + 1)
    for copy in matrices:
        copy.start()

    def columns(owner):
        return pl.ds(pl.multiple_of(owner * 256, 256), 256)

    def send_block(k, i):
        half = lax.div(k, NX)
        there = lax.rem(z + offset(lax.div(i, 2)) + NZ, NZ)
        place = lax.rem(x + lax.rem(k, NX), NX) * 2 + lax.rem(core + lax.rem(i, 2), 2)
        to = there * NE + place
        pltpu.make_async_remote_copy(
            src_ref=x_ref.at[:, half, :, columns(to)],
            dst_ref=field.at[half, z, e, :, :, pl.ds(TS, 2 * TS)],
            send_sem=x_send.at[k],
            recv_sem=x_recv.at[half, x],
            device_id={"lev": to},
            device_id_type=MESH,
        ).start()

    def keep_block(half):
        pltpu.make_async_copy(
            x_ref.at[:, half, :, columns(me)],
            field.at[half, z, e, :, :, pl.ds(TS, 2 * TS)],
            x_recv.at[half, x],
        ).start()

    def send_round(k, first=0):
        def one(i, carry):
            send_block(k, i)
            return carry

        lax.fori_loop(first, 2 * NZ, one, 0)

    send_round(0, 1)
    keep_block(0)
    keep_block(1)
    for k in range(1, WINDOW):
        send_round(k)


    local[3].wait()
    spread = (
        lax.div(lax.broadcasted_iota(jnp.int32, (TS, 1024), 1), 8)
        == lax.broadcasted_iota(jnp.int32, (TS, 1024), 0)
    ).astype(jnp.bfloat16)

    def kron_rows(c, carry):
        rows = (
            c * 16 + lax.div(lax.broadcasted_iota(jnp.int32, (TS, TS), 0), 8)
            == lax.broadcasted_iota(jnp.int32, (TS, TS), 1)
        ).astype(jnp.bfloat16)
        picked = jnp.dot(rows, vert[...], preferred_element_type=jnp.float32).astype(jnp.bfloat16)
        wide = jnp.dot(picked, spread, preferred_element_type=jnp.float32)
        same = lax.rem(lax.broadcasted_iota(jnp.int32, (TS, 1024), 0), 8) == lax.rem(
            lax.broadcasted_iota(jnp.int32, (TS, 1024), 1), 8
        )
        kron[c] = jnp.where(same, wide, 0.0).reshape(NX, 32, 1024).astype(jnp.bfloat16)
        return carry

    lax.fori_loop(0, 8, kron_rows, 0)

    def group(r):
        return lax.rem(x - r + NX, NX)

    def edge(half, g, side):
        rows = (half, slice(None), pl.ds(g * 2, 2), slice(None), slice(None))
        return pltpu.make_async_remote_copy(
            src_ref=field.at[(*rows, pl.ds(TS if side == 0 else 2 * TS, TS))],
            dst_ref=field.at[(*rows, pl.ds(3 * TS if side == 0 else 0, TS))],
            send_sem=e_send.at[half, g, side],
            recv_sem=e_recv.at[half, g, side],
            device_id={"lev": left if side == 0 else right},
            device_id_type=MESH,
        )

    def part(half, g, side):
        return pltpu.make_async_remote_copy(
            src_ref=part_out.at[side, half, g],
            dst_ref=part_in.at[side, half, g],
            send_sem=p_send.at[half, g, side],
            recv_sem=p_recv.at[half, g, side],
            device_id={"col": down if side == 0 else up},
            device_id_type=MESH,
        )

    nt = (((1,), (1,)), ((), ()))

    def answer(half):
        def one_round(r, carry):
            place = lax.rem(x + r, NX)
            rows = kron[:, place].reshape(256, 1024)
            block = jnp.dot(
                rows, mixed[half].reshape(1024, 256), preferred_element_type=jnp.float32
            )
            result[half, :, pl.ds(place * 2, 2)] = block.reshape(NZ, 2, 2, 8, 256).astype(
                jnp.bfloat16
            )

            def send_back(i, inner):
                there = lax.rem(z + offset(lax.div(i, 2)) + NZ, NZ)
                spot = place * 2 + lax.rem(core + lax.rem(i, 2), 2)
                to = there * NE + spot

                @pl.when(to != me)
                def _():
                    pltpu.make_async_remote_copy(
                        src_ref=result.at[half, there, spot],
                        dst_ref=out_ref.at[:, half, :, columns(me)],
                        send_sem=b_send,
                        recv_sem=b_recv,
                        device_id={"lev": to},
                        device_id_type=MESH,
                    ).start()

                @pl.when(to == me)
                def _():
                    pltpu.make_async_copy(
                        result.at[half, z, e], out_ref.at[:, half, :, columns(me)], b_recv
                    ).start()

                return inner

            lax.fori_loop(0, 2 * NZ, send_back, 0)
            return carry

        lax.fori_loop(0, NX, one_round, 0)

    def step(k, carry):
        @pl.when(k < ROUNDS)
        def _():
            half = lax.div(k, NX)
            g = group(lax.rem(k, NX))
            arrived = field.at[half, :, pl.ds(g * 2, 2), :, :, pl.ds(TS, 2 * TS)]
            pltpu.make_async_copy(arrived, arrived, x_recv.at[half, g]).wait()
            edge(half, g, 0).start()
            edge(half, g, 1).start()

        @pl.when(k < ROUNDS - WINDOW)
        def _():
            later = k + WINDOW
            send_round(later, jnp.where(later == NX, 1, 0))

        @pl.when(k == LAG_EDGE)
        def _():
            for copy in matrices:
                copy.wait()

        @pl.when((k >= LAG_EDGE) & (k < ROUNDS + LAG_EDGE))
        def _():
            now = k - LAG_EDGE
            half = lax.div(now, NX)
            g = group(lax.rem(now + 1, NX))
            edge(half, g, 0).wait()
            edge(half, g, 1).wait()
            rows = field[half, :, pl.ds(g * 2, 2)].reshape(256, 4 * TS)
            for side in range(2):
                part_out[side, half, g] = lax.dot_general(
                    rows, weights_in[side], nt, preferred_element_type=jnp.float32
                ).astype(jnp.bfloat16)
                part(half, g, side).start()
            own[half, g] = lax.dot_general(
                rows, weights[1], nt, preferred_element_type=jnp.float32
            )

        @pl.when(k >= LAG_SUM)
        def _():
            now = k - LAG_SUM
            half = lax.div(now, NX)
            g = group(lax.rem(now + 1, NX))
            part(half, g, 0).wait()
            part(half, g, 1).wait()
            total = (
                own[half, g]
                + part_in[0, half, g].astype(jnp.float32)
                + part_in[1, half, g].astype(jnp.float32)
            )
            mixed[half, :, g] = total.reshape(NZ, 32, 256).astype(jnp.bfloat16)

            @pl.when(lax.rem(now, NX) == NX - 1)
            def _():
                answer(half)

        return carry

    lax.fori_loop(0, ROUNDS + LAG_SUM, step, 0)

    for k in range(ROUNDS):
        if k % NX == 0:
            for rows in ((pl.ds(0, NZ - 1), pl.ds(0, 2)), (NZ - 1, pl.ds(0, 1))):
                block = field.at[(0, *rows, slice(None), slice(None), pl.ds(TS, 2 * TS))]
                pltpu.make_async_copy(block, block, x_send.at[k]).wait()
        else:
            block = field.at[0, :, pl.ds(0, 2), :, :, pl.ds(TS, 2 * TS)]
            pltpu.make_async_copy(block, block, x_send.at[k]).wait()
    block = out_ref.at[:, :, :, pl.ds(0, (NL - 1) * 256)]
    pltpu.make_async_copy(block, block, b_send).wait()
    pltpu.make_async_copy(out_ref, out_ref, b_recv).wait()


def body(probe_field, vertical_corr, kernel_tiles, column_tile, tile_counts):
    bf16 = jnp.bfloat16
    dma = pltpu.SemaphoreType.DMA
    any_space = pl.BlockSpec(memory_space=pl.ANY)
    operands = [
        probe_field.reshape(2, 2, 8, NL * 256),
        vertical_corr,
        kernel_tiles.reshape(2, 9, TS, TS),
        column_tile.reshape(2, 9),
        tile_counts,
    ]
    operands = [pltpu.with_memory_space_constraint(a, pltpu.HBM) for a in operands]
    out = pl.pallas_call(
        kernel,
        out_shape=jax.ShapeDtypeStruct((2, 2, 8, NL * 256), bf16),
        in_specs=[any_space] * 5,
        out_specs=any_space,
        scratch_shapes=[
            pltpu.VMEM((2, NZ, NE, 2, 8, 4 * TS), bf16),
            pltpu.VMEM((3, 256, 512), bf16),
            pltpu.VMEM((2, 256, 512), bf16),
            pltpu.VMEM((NZ, NX, 32, 1024), bf16),
            pltpu.VMEM((2, 9, TS, TS), bf16),
            pltpu.VMEM((TS, TS), bf16),
            pltpu.SMEM((2, 9), jnp.int32),
            pltpu.SMEM((1, 2), jnp.int32),
            pltpu.VMEM((2, NX, 256, 256), jnp.float32),
            pltpu.VMEM((2, 2, NX, 256, 256), bf16),
            pltpu.VMEM((2, 2, NX, 256, 256), bf16),
            pltpu.VMEM((2, NZ, NX, 32, 256), bf16),
            pltpu.VMEM((2, NZ, NE, 2, 8, 256), bf16),
            dma((4,)),
            dma((ROUNDS,)),
            dma((2, NX)),
            dma((2, 2)),
            dma((2, 2)),
            dma((2, NX, 2)),
            dma((2, NX, 2)),
            dma((2, NX, 2)),
            dma((2, NX, 2)),
            dma,
            dma,
        ],
        compiler_params=pltpu.CompilerParams(
            collective_id=0, has_side_effects=True, vmem_limit_bytes=40 * 1024 * 1024
        ),
    )(*operands)
    return out.reshape(2, 16, 1, NL * 256)


def solution(mesh):
    placed = (
        P("lev", None, "col", None),
        P(),
        P("col", "lev", None, None, None),
        P("col", "lev", None),
        P("col", "lev"),
    )
    return jax.shard_map(
        body, mesh=mesh, in_specs=placed, out_specs=P("lev", None, "col", None), check_vma=False
    )
```

```python
import jax
import jax.numpy as jnp
from jax import lax
from jax.experimental import pallas as pl
from jax.experimental.pallas import tpu as pltpu
from jax.sharding import PartitionSpec as P

MESH = pl.DeviceIdType.MESH
NZ = 8
NX = 4
NE = 2 * NX
NL = NZ * NE
TS = 128
ENDS = (NE - 1, 0)
ROUNDS = 2 * NX
WINDOW = 3
LAG_EDGE = 2
LAG_SUM = 4


OFFSETS = (0, 1, -1, 2, -2, 3, -3, 4)


def kernel(
    x_ref, v_ref, tiles_ref, slot_hbm, count_hbm, out_ref,
    field, weights, weights_in, kron, tiles, vert, slot_ref, count_ref,
    own, part_out, part_in, mixed, result,
    local_sem, x_send, x_recv, w_send, w_recv,
    t_send, e_send, e_recv, p_send, p_recv, b_send, b_recv,
):
    me = lax.axis_index("lev")
    band = lax.axis_index("col")
    z = lax.div(me, NE)
    e = lax.rem(me, NE)
    x = lax.div(e, 2)
    core = lax.rem(e, 2)
    up = lax.rem(band + 1, 4)
    down = lax.rem(band + 3, 4)
    right = z * NE + lax.rem(e + 1, NE)
    left = z * NE + lax.rem(e + NE - 1, NE)

    barrier = pltpu.get_barrier_semaphore()

    def greet(i, carry):
        pl.semaphore_signal(
            barrier, inc=1, device_id={"lev": lax.rem(me + i, NL)}, device_id_type=MESH
        )
        return carry

    pl.semaphore_signal(barrier, inc=1, device_id={"col": up}, device_id_type=MESH)
    pl.semaphore_signal(barrier, inc=1, device_id={"col": down}, device_id_type=MESH)
    lax.fori_loop(1, NL, greet, 0)

    local = [
        pltpu.make_async_copy(source, target, local_sem.at[i])
        for i, (source, target) in enumerate(
            [(slot_hbm, slot_ref), (count_hbm, count_ref), (tiles_ref, tiles), (v_ref, vert)]
        )
    ]
    for copy in local:
        copy.start()

    for copy in local[:3]:
        copy.wait()
    nothing = jnp.zeros((TS, TS), jnp.bfloat16)
    for t in range(2):
        unused = pl.ds((1 - t) * 3 * TS, TS)
        for side in range(2):
            weights_in[side, t * TS:(t + 1) * TS, unused] = nothing
        weights[1, t * TS:(t + 1) * TS, unused] = nothing
        place = []
        for k in range(9):
            slot = slot_ref[t, k]
            step = lax.div(slot, 128) - band + 1
            shift = lax.rem(lax.rem(slot, 128) - (me * 2 + t) + 129 + 128, 128)
            live = count_ref[0, t] > k
            place.append(jnp.where(live, step * 3 + shift, -1))
        for a in range(3):
            for b in range(3):
                block = jnp.zeros((TS, TS), jnp.float32)
                for k in range(9):
                    hit = jnp.where(place[k] == a * 3 + b, 1.0, 0.0).astype(jnp.float32)
                    block = block + hit * tiles[t, k].astype(jnp.float32)
                weights[a, t * TS:(t + 1) * TS, (t + b) * TS:(t + b + 1) * TS] = block.astype(
                    jnp.bfloat16
                )
    matrices = []
    for side in range(2):
        for t in range(2):
            at = (pl.ds(t * TS, TS), pl.ds(t * TS, 3 * TS))
            matrices.append(
                pltpu.make_async_remote_copy(
                    src_ref=weights.at[(2 - 2 * side, *at)],
                    dst_ref=weights_in.at[(side, *at)],
                    send_sem=w_send.at[side, t],
                    recv_sem=w_recv.at[side, t],
                    device_id={"col": down if side else up},
                    device_id_type=MESH,
                )
            )

    pl.semaphore_wait(barrier, NL + 1)
    for copy in matrices:
        copy.start()

    def columns(owner):
        return pl.ds(pl.multiple_of(owner * 256, 256), 256)

    planes = [lax.rem(z + step + NZ, NZ) for step in OFFSETS]

    def send_block(k, i):
        half = lax.div(k, NX)
        place = lax.rem(x + lax.rem(k, NX), NX) * 2 + (core if i % 2 == 0 else 1 - core)
        to = planes[i // 2] * NE + place
        pltpu.make_async_remote_copy(
            src_ref=x_ref.at[:, half, :, columns(to)],
            dst_ref=field.at[half, z, e, :, :, pl.ds(TS, 2 * TS)],
            send_sem=x_send.at[k],
            recv_sem=x_recv.at[half, x],
            device_id={"lev": to},
            device_id_type=MESH,
        ).start()

    def tile_ends(k, i, side):
        half = lax.div(k, NX)
        owner = planes[i] * NE + ENDS[side]
        beyond = lax.rem(owner * 2 + (2 if side == 0 else 127), 128)
        return (
            x_ref.at[:, half, :, pl.ds(pl.multiple_of(beyond * TS, TS), TS)],
            field.at[half, z, e, :, :, pl.ds(3 * TS if side == 0 else 0, TS)],
            e_recv.at[half, x, side],
        )

    def send_tile(k, i, side):
        source, target, arrived = tile_ends(k, i, side)
        pltpu.make_async_remote_copy(
            src_ref=source,
            dst_ref=target,
            send_sem=t_send.at[lax.div(k, NX), side],
            recv_sem=arrived,
            device_id={"lev": planes[i] * NE + ENDS[side]},
            device_id_type=MESH,
        ).start()

    def keep_block(half):
        pltpu.make_async_copy(
            x_ref.at[:, half, :, columns(me)],
            field.at[half, z, e, :, :, pl.ds(TS, 2 * TS)],
            x_recv.at[half, x],
        ).start()

    def send_round(k):
        for i in range(1, 2 * NZ):
            send_block(k, i)

        @pl.when(lax.rem(k, NX) != 0)
        def _():
            send_block(k, 0)

        for side in range(2):
            @pl.when(lax.rem(x + k, NX) == (NX - 1 if side == 0 else 0))
            def _():
                for i in range(1, NZ):
                    send_tile(k, i, side)

                @pl.when(e != ENDS[side])
                def _():
                    send_tile(k, 0, side)

                @pl.when(e == ENDS[side])
                def _():
                    source, target, arrived = tile_ends(k, 0, side)
                    pltpu.make_async_copy(source, target, arrived).start()

    def first_rounds(k, carry):
        send_round(k)
        return carry

    lax.fori_loop(0, WINDOW, first_rounds, 0)
    keep_block(0)
    keep_block(1)


    local[3].wait()
    spread = (
        lax.div(lax.broadcasted_iota(jnp.int32, (TS, 1024), 1), 8)
        == lax.broadcasted_iota(jnp.int32, (TS, 1024), 0)
    ).astype(jnp.bfloat16)

    def kron_rows(c, carry):
        rows = (
            c * 16 + lax.div(lax.broadcasted_iota(jnp.int32, (TS, TS), 0), 8)
            == lax.broadcasted_iota(jnp.int32, (TS, TS), 1)
        ).astype(jnp.bfloat16)
        picked = jnp.dot(rows, vert[...], preferred_element_type=jnp.float32).astype(jnp.bfloat16)
        wide = jnp.dot(picked, spread, preferred_element_type=jnp.float32)
        same = lax.rem(lax.broadcasted_iota(jnp.int32, (TS, 1024), 0), 8) == lax.rem(
            lax.broadcasted_iota(jnp.int32, (TS, 1024), 1), 8
        )
        kron[c] = jnp.where(same, wide, 0.0).reshape(NX, 32, 1024).astype(jnp.bfloat16)
        return carry

    lax.fori_loop(0, 8, kron_rows, 0)

    def group(r):
        return lax.rem(x - r + NX, NX)

    def edge(half, g, side):
        rows = (half, slice(None), pl.ds(g * 2, 2), slice(None), slice(None))
        return pltpu.make_async_remote_copy(
            src_ref=field.at[(*rows, pl.ds(TS if side == 0 else 2 * TS, TS))],
            dst_ref=field.at[(*rows, pl.ds(3 * TS if side == 0 else 0, TS))],
            send_sem=e_send.at[half, g, side],
            recv_sem=e_recv.at[half, g, side],
            device_id={"lev": left if side == 0 else right},
            device_id_type=MESH,
        )

    def part(half, g, side):
        return pltpu.make_async_remote_copy(
            src_ref=part_out.at[side, half, g],
            dst_ref=part_in.at[side, half, g],
            send_sem=p_send.at[half, g, side],
            recv_sem=p_recv.at[half, g, side],
            device_id={"col": down if side == 0 else up},
            device_id_type=MESH,
        )

    nt = (((1,), (1,)), ((), ()))

    def answer(half):
        def one_round(r, carry):
            place = lax.rem(x + r, NX)
            rows = kron[:, place].reshape(256, 1024)
            block = jnp.dot(
                rows, mixed[half].reshape(1024, 256), preferred_element_type=jnp.float32
            )
            result[half, :, pl.ds(place * 2, 2)] = block.reshape(NZ, 2, 2, 8, 256).astype(
                jnp.bfloat16
            )

            def send_back(i):
                spot = place * 2 + (core if i % 2 == 0 else 1 - core)
                to = planes[i // 2] * NE + spot
                pltpu.make_async_remote_copy(
                    src_ref=result.at[half, planes[i // 2], spot],
                    dst_ref=out_ref.at[:, half, :, columns(me)],
                    send_sem=b_send,
                    recv_sem=b_recv,
                    device_id={"lev": to},
                    device_id_type=MESH,
                ).start()

            for i in range(1, 2 * NZ):
                send_back(i)

            @pl.when(r != 0)
            def _():
                send_back(0)

            @pl.when(r == 0)
            def _():
                pltpu.make_async_copy(
                    result.at[half, z, e], out_ref.at[:, half, :, columns(me)], b_recv
                ).start()
            return carry

        lax.fori_loop(0, NX, one_round, 0)

    def step(k, carry):
        @pl.when(k < ROUNDS)
        def _():
            half = lax.div(k, NX)
            g = group(lax.rem(k, NX))
            arrived = field.at[half, :, pl.ds(g * 2, 2), :, :, pl.ds(TS, 2 * TS)]
            pltpu.make_async_copy(arrived, arrived, x_recv.at[half, g]).wait()

            @pl.when(e != 0)
            def _():
                edge(half, g, 0).start()

            @pl.when(e != NE - 1)
            def _():
                edge(half, g, 1).start()

        @pl.when(k < ROUNDS - WINDOW)
        def _():
            send_round(k + WINDOW)

        @pl.when(k == LAG_EDGE)
        def _():
            for copy in matrices:
                copy.wait()

        @pl.when((k >= LAG_EDGE) & (k < ROUNDS + LAG_EDGE))
        def _():
            now = k - LAG_EDGE
            half = lax.div(now, NX)
            g = group(lax.rem(now + 1, NX))
            edge(half, g, 0).wait_recv()
            edge(half, g, 1).wait_recv()
            rows = field[half, :, pl.ds(g * 2, 2)].reshape(256, 4 * TS)
            for side in range(2):
                part_out[side, half, g] = lax.dot_general(
                    rows, weights_in[side], nt, preferred_element_type=jnp.float32
                ).astype(jnp.bfloat16)
                part(half, g, side).start()
            own[half, g] = lax.dot_general(
                rows, weights[1], nt, preferred_element_type=jnp.float32
            )

        @pl.when(k >= LAG_SUM)
        def _():
            now = k - LAG_SUM
            half = lax.div(now, NX)
            g = group(lax.rem(now + 1, NX))
            part(half, g, 0).wait()
            part(half, g, 1).wait()
            total = (
                own[half, g]
                + part_in[0, half, g].astype(jnp.float32)
                + part_in[1, half, g].astype(jnp.float32)
            )
            mixed[half, :, g] = total.reshape(NZ, 32, 256).astype(jnp.bfloat16)

            @pl.when(lax.rem(now, NX) == NX - 1)
            def _():
                answer(half)

        return carry

    lax.fori_loop(0, ROUNDS + LAG_SUM, step, 0)

    for k in range(ROUNDS):
        if k % NX == 0:
            for rows in ((pl.ds(0, NZ - 1), pl.ds(0, 2)), (NZ - 1, pl.ds(0, 1))):
                block = field.at[(0, *rows, slice(None), slice(None), pl.ds(TS, 2 * TS))]
                pltpu.make_async_copy(block, block, x_send.at[k]).wait()
        else:
            block = field.at[0, :, pl.ds(0, 2), :, :, pl.ds(TS, 2 * TS)]
            pltpu.make_async_copy(block, block, x_send.at[k]).wait()
    for half in range(2):
        for side in range(2):
            block = field.at[half, pl.ds(0, NZ - 1), 0, :, :, pl.ds(0, TS)]
            pltpu.make_async_copy(block, block, t_send.at[half, side]).wait()

            @pl.when(e != ENDS[side])
            def _():
                block = field.at[half, 0, 0, :, :, pl.ds(0, TS)]
                pltpu.make_async_copy(block, block, t_send.at[half, side]).wait()

            @pl.when(e != (0 if side == 0 else NE - 1))
            def _():
                for g in range(NX):
                    edge(half, g, side).wait_send()

    block = out_ref.at[:, :, :, pl.ds(0, (NL - 1) * 256)]
    pltpu.make_async_copy(block, block, b_send).wait()
    pltpu.make_async_copy(out_ref, out_ref, b_recv).wait()


def body(probe_field, vertical_corr, kernel_tiles, column_tile, tile_counts):
    bf16 = jnp.bfloat16
    dma = pltpu.SemaphoreType.DMA
    any_space = pl.BlockSpec(memory_space=pl.ANY)
    operands = [
        probe_field.reshape(2, 2, 8, NL * 256),
        vertical_corr,
        kernel_tiles.reshape(2, 9, TS, TS),
        column_tile.reshape(2, 9),
        tile_counts,
    ]
    operands = [pltpu.with_memory_space_constraint(a, pltpu.HBM) for a in operands]
    out = pl.pallas_call(
        kernel,
        out_shape=jax.ShapeDtypeStruct((2, 2, 8, NL * 256), bf16),
        in_specs=[any_space] * 5,
        out_specs=any_space,
        scratch_shapes=[
            pltpu.VMEM((2, NZ, NE, 2, 8, 4 * TS), bf16),
            pltpu.VMEM((3, 256, 512), bf16),
            pltpu.VMEM((2, 256, 512), bf16),
            pltpu.VMEM((NZ, NX, 32, 1024), bf16),
            pltpu.VMEM((2, 9, TS, TS), bf16),
            pltpu.VMEM((TS, TS), bf16),
            pltpu.SMEM((2, 9), jnp.int32),
            pltpu.SMEM((1, 2), jnp.int32),
            pltpu.VMEM((2, NX, 256, 256), jnp.float32),
            pltpu.VMEM((2, 2, NX, 256, 256), bf16),
            pltpu.VMEM((2, 2, NX, 256, 256), bf16),
            pltpu.VMEM((2, NZ, NX, 32, 256), bf16),
            pltpu.VMEM((2, NZ, NE, 2, 8, 256), bf16),
            dma((4,)),
            dma((ROUNDS,)),
            dma((2, NX)),
            dma((2, 2)),
            dma((2, 2)),
            dma((2, 2)),
            dma((2, NX, 2)),
            dma((2, NX, 2)),
            dma((2, NX, 2)),
            dma((2, NX, 2)),
            dma,
            dma,
        ],
        compiler_params=pltpu.CompilerParams(
            collective_id=0, has_side_effects=True, vmem_limit_bytes=40 * 1024 * 1024
        ),
    )(*operands)
    return out.reshape(2, 16, 1, NL * 256)


def solution(mesh):
    placed = (
        P("lev", None, "col", None),
        P(),
        P("col", "lev", None, None, None),
        P("col", "lev", None),
        P("col", "lev"),
    )
    return jax.shard_map(
        body, mesh=mesh, in_specs=placed, out_specs=P("lev", None, "col", None), check_vma=False
    )
```

```python
import jax
import jax.numpy as jnp
from jax import lax
from jax.experimental import pallas as pl
from jax.experimental.pallas import tpu as pltpu
from jax.sharding import PartitionSpec as P

MESH = pl.DeviceIdType.MESH
NZ = 8
NX = 4
NE = 2 * NX
NL = NZ * NE
TS = 128
ENDS = (NE - 1, 0)
ROUNDS = 2 * NX
WINDOW = 3
LAG_EDGE = 2
LAG_SUM = 4


OFFSETS = (0, 4, 3, -3, 2, -2, 1, -1)


def kernel(
    x_ref, v_ref, tiles_ref, slot_hbm, count_hbm, out_ref,
    field, weights, weights_in, kron, tiles, vert, slot_ref, count_ref,
    own, part_out, part_in, mixed, result,
    local_sem, x_send, x_recv, w_send, w_recv,
    t_send, e_send, e_recv, p_send, p_recv, b_send, b_recv,
):
    me = lax.axis_index("lev")
    band = lax.axis_index("col")
    z = lax.div(me, NE)
    e = lax.rem(me, NE)
    x = lax.div(e, 2)
    core = lax.rem(e, 2)
    up = lax.rem(band + 1, 4)
    down = lax.rem(band + 3, 4)
    right = z * NE + lax.rem(e + 1, NE)
    left = z * NE + lax.rem(e + NE - 1, NE)

    barrier = pltpu.get_barrier_semaphore()

    def greet(i, carry):
        pl.semaphore_signal(
            barrier, inc=1, device_id={"lev": lax.rem(me + i, NL)}, device_id_type=MESH
        )
        return carry

    pl.semaphore_signal(barrier, inc=1, device_id={"col": up}, device_id_type=MESH)
    pl.semaphore_signal(barrier, inc=1, device_id={"col": down}, device_id_type=MESH)
    lax.fori_loop(1, NL, greet, 0)

    local = [
        pltpu.make_async_copy(source, target, local_sem.at[i])
        for i, (source, target) in enumerate(
            [(slot_hbm, slot_ref), (count_hbm, count_ref), (tiles_ref, tiles), (v_ref, vert)]
        )
    ]
    for copy in local:
        copy.start()

    for copy in local[:3]:
        copy.wait()
    nothing = jnp.zeros((TS, TS), jnp.bfloat16)
    for t in range(2):
        unused = pl.ds((1 - t) * 3 * TS, TS)
        for side in range(2):
            weights_in[side, t * TS:(t + 1) * TS, unused] = nothing
        weights[1, t * TS:(t + 1) * TS, unused] = nothing
        place = []
        for k in range(9):
            slot = slot_ref[t, k]
            step = lax.div(slot, 128) - band + 1
            shift = lax.rem(lax.rem(slot, 128) - (me * 2 + t) + 129 + 128, 128)
            live = count_ref[0, t] > k
            place.append(jnp.where(live, step * 3 + shift, -1))
        for a in range(3):
            for b in range(3):
                block = jnp.zeros((TS, TS), jnp.float32)
                for k in range(9):
                    hit = jnp.where(place[k] == a * 3 + b, 1.0, 0.0).astype(jnp.float32)
                    block = block + hit * tiles[t, k].astype(jnp.float32)
                weights[a, t * TS:(t + 1) * TS, (t + b) * TS:(t + b + 1) * TS] = block.astype(
                    jnp.bfloat16
                )
    matrices = []
    for side in range(2):
        for t in range(2):
            at = (pl.ds(t * TS, TS), pl.ds(t * TS, 3 * TS))
            matrices.append(
                pltpu.make_async_remote_copy(
                    src_ref=weights.at[(2 - 2 * side, *at)],
                    dst_ref=weights_in.at[(side, *at)],
                    send_sem=w_send.at[side, t],
                    recv_sem=w_recv.at[side, t],
                    device_id={"col": down if side else up},
                    device_id_type=MESH,
                )
            )

    pl.semaphore_wait(barrier, NL + 1)
    for copy in matrices:
        copy.start()

    def columns(owner):
        return pl.ds(pl.multiple_of(owner * 256, 256), 256)

    planes = [lax.rem(z + step + NZ, NZ) for step in OFFSETS]

    def send_block(k, i):
        half = lax.div(k, NX)
        place = lax.rem(x + lax.rem(k, NX), NX) * 2 + (core if i % 2 == 0 else 1 - core)
        to = planes[i // 2] * NE + place
        pltpu.make_async_remote_copy(
            src_ref=x_ref.at[:, half, :, columns(to)],
            dst_ref=field.at[half, z, e, :, :, pl.ds(TS, 2 * TS)],
            send_sem=x_send.at[k],
            recv_sem=x_recv.at[half, x],
            device_id={"lev": to},
            device_id_type=MESH,
        ).start()

    def tile_ends(k, i, side):
        half = lax.div(k, NX)
        owner = planes[i] * NE + ENDS[side]
        beyond = lax.rem(owner * 2 + (2 if side == 0 else 127), 128)
        return (
            x_ref.at[:, half, :, pl.ds(pl.multiple_of(beyond * TS, TS), TS)],
            field.at[half, z, e, :, :, pl.ds(3 * TS if side == 0 else 0, TS)],
            e_recv.at[half, x, side],
        )

    def send_tile(k, i, side):
        source, target, arrived = tile_ends(k, i, side)
        pltpu.make_async_remote_copy(
            src_ref=source,
            dst_ref=target,
            send_sem=t_send.at[lax.div(k, NX), side],
            recv_sem=arrived,
            device_id={"lev": planes[i] * NE + ENDS[side]},
            device_id_type=MESH,
        ).start()

    def keep_block(half):
        pltpu.make_async_copy(
            x_ref.at[:, half, :, columns(me)],
            field.at[half, z, e, :, :, pl.ds(TS, 2 * TS)],
            x_recv.at[half, x],
        ).start()

    def send_round(k):
        for i in (*range(2, 2 * NZ), 1):
            send_block(k, i)

        @pl.when(lax.rem(k, NX) != 0)
        def _():
            send_block(k, 0)

        for side in range(2):
            @pl.when(lax.rem(x + k, NX) == (NX - 1 if side == 0 else 0))
            def _():
                for i in range(1, NZ):
                    send_tile(k, i, side)

                @pl.when(e != ENDS[side])
                def _():
                    send_tile(k, 0, side)

                @pl.when(e == ENDS[side])
                def _():
                    source, target, arrived = tile_ends(k, 0, side)
                    pltpu.make_async_copy(source, target, arrived).start()

    def first_rounds(k, carry):
        send_round(k)
        return carry

    lax.fori_loop(0, WINDOW, first_rounds, 0)
    keep_block(0)
    keep_block(1)


    local[3].wait()
    spread = (
        lax.div(lax.broadcasted_iota(jnp.int32, (TS, 1024), 1), 8)
        == lax.broadcasted_iota(jnp.int32, (TS, 1024), 0)
    ).astype(jnp.bfloat16)

    def kron_rows(c, carry):
        rows = (
            c * 16 + lax.div(lax.broadcasted_iota(jnp.int32, (TS, TS), 0), 8)
            == lax.broadcasted_iota(jnp.int32, (TS, TS), 1)
        ).astype(jnp.bfloat16)
        picked = jnp.dot(rows, vert[...], preferred_element_type=jnp.float32).astype(jnp.bfloat16)
        wide = jnp.dot(picked, spread, preferred_element_type=jnp.float32)
        same = lax.rem(lax.broadcasted_iota(jnp.int32, (TS, 1024), 0), 8) == lax.rem(
            lax.broadcasted_iota(jnp.int32, (TS, 1024), 1), 8
        )
        kron[c] = jnp.where(same, wide, 0.0).reshape(NX, 32, 1024).astype(jnp.bfloat16)
        return carry

    lax.fori_loop(0, 8, kron_rows, 0)

    def group(r):
        return lax.rem(x - r + NX, NX)

    def edge(half, g, side):
        rows = (half, slice(None), pl.ds(g * 2, 2), slice(None), slice(None))
        return pltpu.make_async_remote_copy(
            src_ref=field.at[(*rows, pl.ds(TS if side == 0 else 2 * TS, TS))],
            dst_ref=field.at[(*rows, pl.ds(3 * TS if side == 0 else 0, TS))],
            send_sem=e_send.at[half, g, side],
            recv_sem=e_recv.at[half, g, side],
            device_id={"lev": left if side == 0 else right},
            device_id_type=MESH,
        )

    def part(half, g, side):
        return pltpu.make_async_remote_copy(
            src_ref=part_out.at[side, half, g],
            dst_ref=part_in.at[side, half, g],
            send_sem=p_send.at[half, g, side],
            recv_sem=p_recv.at[half, g, side],
            device_id={"col": down if side == 0 else up},
            device_id_type=MESH,
        )

    nt = (((1,), (1,)), ((), ()))

    def answer(half):
        def one_round(r, carry):
            place = lax.rem(x + r + 1, NX)
            rows = kron[:, place].reshape(256, 1024)
            block = jnp.dot(
                rows, mixed[half].reshape(1024, 256), preferred_element_type=jnp.float32
            )
            result[half, :, pl.ds(place * 2, 2)] = block.reshape(NZ, 2, 2, 8, 256).astype(
                jnp.bfloat16
            )

            def send_back(i):
                spot = place * 2 + (core if i % 2 == 0 else 1 - core)
                to = planes[i // 2] * NE + spot
                pltpu.make_async_remote_copy(
                    src_ref=result.at[half, planes[i // 2], spot],
                    dst_ref=out_ref.at[:, half, :, columns(me)],
                    send_sem=b_send,
                    recv_sem=b_recv,
                    device_id={"lev": to},
                    device_id_type=MESH,
                ).start()

            for i in (*range(2, 2 * NZ), 1):
                send_back(i)

            @pl.when(r != NX - 1)
            def _():
                send_back(0)

            @pl.when(r == NX - 1)
            def _():
                pltpu.make_async_copy(
                    result.at[half, z, e], out_ref.at[:, half, :, columns(me)], b_recv
                ).start()
            return carry

        lax.fori_loop(0, NX, one_round, 0)

    def step(k, carry):
        @pl.when(k < ROUNDS)
        def _():
            half = lax.div(k, NX)
            g = group(lax.rem(k, NX))
            arrived = field.at[half, :, pl.ds(g * 2, 2), :, :, pl.ds(TS, 2 * TS)]
            pltpu.make_async_copy(arrived, arrived, x_recv.at[half, g]).wait()

            @pl.when(e != 0)
            def _():
                edge(half, g, 0).start()

            @pl.when(e != NE - 1)
            def _():
                edge(half, g, 1).start()

        @pl.when(k < ROUNDS - WINDOW)
        def _():
            send_round(k + WINDOW)

        @pl.when(k == LAG_EDGE)
        def _():
            for copy in matrices:
                copy.wait()

        @pl.when((k >= LAG_EDGE) & (k < ROUNDS + LAG_EDGE))
        def _():
            now = k - LAG_EDGE
            half = lax.div(now, NX)
            g = group(lax.rem(now + 1, NX))
            edge(half, g, 0).wait_recv()
            edge(half, g, 1).wait_recv()
            rows = field[half, :, pl.ds(g * 2, 2)].reshape(256, 4 * TS)
            for side in range(2):
                part_out[side, half, g] = lax.dot_general(
                    rows, weights_in[side], nt, preferred_element_type=jnp.float32
                ).astype(jnp.bfloat16)
                part(half, g, side).start()
            own[half, g] = lax.dot_general(
                rows, weights[1], nt, preferred_element_type=jnp.float32
            )

        @pl.when(k >= LAG_SUM)
        def _():
            now = k - LAG_SUM
            half = lax.div(now, NX)
            g = group(lax.rem(now + 1, NX))
            part(half, g, 0).wait()
            part(half, g, 1).wait()
            total = (
                own[half, g]
                + part_in[0, half, g].astype(jnp.float32)
                + part_in[1, half, g].astype(jnp.float32)
            )
            mixed[half, :, g] = total.reshape(NZ, 32, 256).astype(jnp.bfloat16)

            @pl.when(lax.rem(now, NX) == NX - 1)
            def _():
                answer(half)

        return carry

    lax.fori_loop(0, ROUNDS + LAG_SUM, step, 0)

    for k in range(ROUNDS):
        if k % NX == 0:
            for rows in ((pl.ds(0, NZ - 1), pl.ds(0, 2)), (NZ - 1, pl.ds(0, 1))):
                block = field.at[(0, *rows, slice(None), slice(None), pl.ds(TS, 2 * TS))]
                pltpu.make_async_copy(block, block, x_send.at[k]).wait()
        else:
            block = field.at[0, :, pl.ds(0, 2), :, :, pl.ds(TS, 2 * TS)]
            pltpu.make_async_copy(block, block, x_send.at[k]).wait()
    for half in range(2):
        for side in range(2):
            block = field.at[half, pl.ds(0, NZ - 1), 0, :, :, pl.ds(0, TS)]
            pltpu.make_async_copy(block, block, t_send.at[half, side]).wait()

            @pl.when(e != ENDS[side])
            def _():
                block = field.at[half, 0, 0, :, :, pl.ds(0, TS)]
                pltpu.make_async_copy(block, block, t_send.at[half, side]).wait()

            @pl.when(e != (0 if side == 0 else NE - 1))
            def _():
                for g in range(NX):
                    edge(half, g, side).wait_send()

    block = out_ref.at[:, :, :, pl.ds(0, (NL - 1) * 256)]
    pltpu.make_async_copy(block, block, b_send).wait()
    pltpu.make_async_copy(out_ref, out_ref, b_recv).wait()


def body(probe_field, vertical_corr, kernel_tiles, column_tile, tile_counts):
    bf16 = jnp.bfloat16
    dma = pltpu.SemaphoreType.DMA
    any_space = pl.BlockSpec(memory_space=pl.ANY)
    operands = [
        probe_field.reshape(2, 2, 8, NL * 256),
        vertical_corr,
        kernel_tiles.reshape(2, 9, TS, TS),
        column_tile.reshape(2, 9),
        tile_counts,
    ]
    operands = [pltpu.with_memory_space_constraint(a, pltpu.HBM) for a in operands]
    out = pl.pallas_call(
        kernel,
        out_shape=jax.ShapeDtypeStruct((2, 2, 8, NL * 256), bf16),
        in_specs=[any_space] * 5,
        out_specs=any_space,
        scratch_shapes=[
            pltpu.VMEM((2, NZ, NE, 2, 8, 4 * TS), bf16),
            pltpu.VMEM((3, 256, 512), bf16),
            pltpu.VMEM((2, 256, 512), bf16),
            pltpu.VMEM((NZ, NX, 32, 1024), bf16),
            pltpu.VMEM((2, 9, TS, TS), bf16),
            pltpu.VMEM((TS, TS), bf16),
            pltpu.SMEM((2, 9), jnp.int32),
            pltpu.SMEM((1, 2), jnp.int32),
            pltpu.VMEM((2, NX, 256, 256), jnp.float32),
            pltpu.VMEM((2, 2, NX, 256, 256), bf16),
            pltpu.VMEM((2, 2, NX, 256, 256), bf16),
            pltpu.VMEM((2, NZ, NX, 32, 256), bf16),
            pltpu.VMEM((2, NZ, NE, 2, 8, 256), bf16),
            dma((4,)),
            dma((ROUNDS,)),
            dma((2, NX)),
            dma((2, 2)),
            dma((2, 2)),
            dma((2, 2)),
            dma((2, NX, 2)),
            dma((2, NX, 2)),
            dma((2, NX, 2)),
            dma((2, NX, 2)),
            dma,
            dma,
        ],
        compiler_params=pltpu.CompilerParams(
            collective_id=0, has_side_effects=True, vmem_limit_bytes=40 * 1024 * 1024
        ),
    )(*operands)
    return out.reshape(2, 16, 1, NL * 256)


def solution(mesh):
    placed = (
        P("lev", None, "col", None),
        P(),
        P("col", "lev", None, None, None),
        P("col", "lev", None),
        P("col", "lev"),
    )
    return jax.shard_map(
        body, mesh=mesh, in_specs=placed, out_specs=P("lev", None, "col", None), check_vma=False
    )
```

```python
import jax
import jax.numpy as jnp
from jax import lax
from jax.experimental import pallas as pl
from jax.experimental.pallas import tpu as pltpu
from jax.sharding import PartitionSpec as P

MESH = pl.DeviceIdType.MESH
NZ = 8
NX = 4
NE = 2 * NX
NL = NZ * NE
TS = 128
ENDS = (NE - 1, 0)
ROUNDS = 2 * NX
WINDOW = 4
LAG_EDGE = 2
LAG_SUM = 4


OFFSETS = (0, 4, 3, -3, 2, -2, 1, -1)


def kernel(
    x_ref, v_ref, tiles_ref, slot_hbm, count_hbm, out_ref,
    field, weights, weights_in, kron, tiles, vert, slot_ref, count_ref,
    own, part_out, part_in, mixed, result,
    local_sem, x_send, x_recv, w_send, w_recv,
    t_send, e_send, e_recv, p_send, p_recv, b_send, b_recv,
):
    me = lax.axis_index("lev")
    band = lax.axis_index("col")
    z = lax.div(me, NE)
    e = lax.rem(me, NE)
    x = lax.div(e, 2)
    core = lax.rem(e, 2)
    up = lax.rem(band + 1, 4)
    down = lax.rem(band + 3, 4)
    right = z * NE + lax.rem(e + 1, NE)
    left = z * NE + lax.rem(e + NE - 1, NE)

    barrier = pltpu.get_barrier_semaphore()

    def greet(i, carry):
        pl.semaphore_signal(
            barrier, inc=1, device_id={"lev": lax.rem(me + i, NL)}, device_id_type=MESH
        )
        return carry

    pl.semaphore_signal(barrier, inc=1, device_id={"col": up}, device_id_type=MESH)
    pl.semaphore_signal(barrier, inc=1, device_id={"col": down}, device_id_type=MESH)
    lax.fori_loop(1, NL, greet, 0)

    local = [
        pltpu.make_async_copy(source, target, local_sem.at[i])
        for i, (source, target) in enumerate(
            [(slot_hbm, slot_ref), (count_hbm, count_ref), (tiles_ref, tiles), (v_ref, vert)]
        )
    ]
    for copy in local:
        copy.start()

    for copy in local[:3]:
        copy.wait()
    nothing = jnp.zeros((TS, TS), jnp.bfloat16)
    for t in range(2):
        unused = pl.ds((1 - t) * 3 * TS, TS)
        for side in range(2):
            weights_in[side, t * TS:(t + 1) * TS, unused] = nothing
        weights[1, t * TS:(t + 1) * TS, unused] = nothing
        place = []
        for k in range(9):
            slot = slot_ref[t, k]
            step = lax.div(slot, 128) - band + 1
            shift = lax.rem(lax.rem(slot, 128) - (me * 2 + t) + 129 + 128, 128)
            live = count_ref[0, t] > k
            place.append(jnp.where(live, step * 3 + shift, -1))
        for a in range(3):
            for b in range(3):
                block = jnp.zeros((TS, TS), jnp.float32)
                for k in range(9):
                    hit = jnp.where(place[k] == a * 3 + b, 1.0, 0.0).astype(jnp.float32)
                    block = block + hit * tiles[t, k].astype(jnp.float32)
                weights[a, t * TS:(t + 1) * TS, (t + b) * TS:(t + b + 1) * TS] = block.astype(
                    jnp.bfloat16
                )
    matrices = []
    for side in range(2):
        for t in range(2):
            at = (pl.ds(t * TS, TS), pl.ds(t * TS, 3 * TS))
            matrices.append(
                pltpu.make_async_remote_copy(
                    src_ref=weights.at[(2 - 2 * side, *at)],
                    dst_ref=weights_in.at[(side, *at)],
                    send_sem=w_send.at[side, t],
                    recv_sem=w_recv.at[side, t],
                    device_id={"col": down if side else up},
                    device_id_type=MESH,
                )
            )

    pl.semaphore_wait(barrier, NL + 1)
    for copy in matrices:
        copy.start()

    def columns(owner):
        return pl.ds(pl.multiple_of(owner * 256, 256), 256)

    planes = [lax.rem(z + step + NZ, NZ) for step in OFFSETS]

    def send_block(k, i):
        half = lax.div(k, NX)
        place = lax.rem(x + lax.rem(k, NX), NX) * 2 + (core if i % 2 == 0 else 1 - core)
        to = planes[i // 2] * NE + place
        pltpu.make_async_remote_copy(
            src_ref=x_ref.at[:, half, :, columns(to)],
            dst_ref=field.at[half, z, e, :, :, pl.ds(TS, 2 * TS)],
            send_sem=x_send.at[k],
            recv_sem=x_recv.at[half, x],
            device_id={"lev": to},
            device_id_type=MESH,
        ).start()

    def tile_ends(k, i, side):
        half = lax.div(k, NX)
        owner = planes[i] * NE + ENDS[side]
        beyond = lax.rem(owner * 2 + (2 if side == 0 else 127), 128)
        return (
            x_ref.at[:, half, :, pl.ds(pl.multiple_of(beyond * TS, TS), TS)],
            field.at[half, z, e, :, :, pl.ds(3 * TS if side == 0 else 0, TS)],
            e_recv.at[half, x, side],
        )

    def send_tile(k, i, side):
        source, target, arrived = tile_ends(k, i, side)
        pltpu.make_async_remote_copy(
            src_ref=source,
            dst_ref=target,
            send_sem=t_send.at[lax.div(k, NX), side],
            recv_sem=arrived,
            device_id={"lev": planes[i] * NE + ENDS[side]},
            device_id_type=MESH,
        ).start()

    def keep_block(half):
        pltpu.make_async_copy(
            x_ref.at[:, half, :, columns(me)],
            field.at[half, z, e, :, :, pl.ds(TS, 2 * TS)],
            x_recv.at[half, x],
        ).start()

    def send_round(k):
        for i in (*range(2, 2 * NZ), 1):
            send_block(k, i)

        @pl.when(lax.rem(k, NX) != 0)
        def _():
            send_block(k, 0)

        for side in range(2):
            @pl.when(lax.rem(x + k, NX) == (NX - 1 if side == 0 else 0))
            def _():
                for i in range(1, NZ):
                    send_tile(k, i, side)

                @pl.when(e != ENDS[side])
                def _():
                    send_tile(k, 0, side)

                @pl.when(e == ENDS[side])
                def _():
                    source, target, arrived = tile_ends(k, 0, side)
                    pltpu.make_async_copy(source, target, arrived).start()

    def first_rounds(k, carry):
        send_round(k)
        return carry

    lax.fori_loop(0, WINDOW, first_rounds, 0)
    keep_block(0)
    keep_block(1)


    local[3].wait()
    spread = (
        lax.div(lax.broadcasted_iota(jnp.int32, (TS, 1024), 1), 8)
        == lax.broadcasted_iota(jnp.int32, (TS, 1024), 0)
    ).astype(jnp.bfloat16)

    def kron_rows(c, carry):
        rows = (
            c * 16 + lax.div(lax.broadcasted_iota(jnp.int32, (TS, TS), 0), 8)
            == lax.broadcasted_iota(jnp.int32, (TS, TS), 1)
        ).astype(jnp.bfloat16)
        picked = jnp.dot(rows, vert[...], preferred_element_type=jnp.float32).astype(jnp.bfloat16)
        wide = jnp.dot(picked, spread, preferred_element_type=jnp.float32)
        same = lax.rem(lax.broadcasted_iota(jnp.int32, (TS, 1024), 0), 8) == lax.rem(
            lax.broadcasted_iota(jnp.int32, (TS, 1024), 1), 8
        )
        kron[c] = jnp.where(same, wide, 0.0).reshape(NX, 32, 1024).astype(jnp.bfloat16)
        return carry

    lax.fori_loop(0, 8, kron_rows, 0)

    def group(r):
        return lax.rem(x - r + NX, NX)

    def edge(half, g, side):
        rows = (half, slice(None), pl.ds(g * 2, 2), slice(None), slice(None))
        return pltpu.make_async_remote_copy(
            src_ref=field.at[(*rows, pl.ds(TS if side == 0 else 2 * TS, TS))],
            dst_ref=field.at[(*rows, pl.ds(3 * TS if side == 0 else 0, TS))],
            send_sem=e_send.at[half, g, side],
            recv_sem=e_recv.at[half, g, side],
            device_id={"lev": left if side == 0 else right},
            device_id_type=MESH,
        )

    def part(half, g, side):
        return pltpu.make_async_remote_copy(
            src_ref=part_out.at[side, half, g],
            dst_ref=part_in.at[side, half, g],
            send_sem=p_send.at[half, g, side],
            recv_sem=p_recv.at[half, g, side],
            device_id={"col": down if side == 0 else up},
            device_id_type=MESH,
        )

    nt = (((1,), (1,)), ((), ()))

    def answer(half):
        def one_round(r, carry):
            place = lax.rem(x + r + 1, NX)
            rows = kron[:, place].reshape(256, 1024)
            block = jnp.dot(
                rows, mixed[half].reshape(1024, 256), preferred_element_type=jnp.float32
            )
            result[half, :, pl.ds(place * 2, 2)] = block.reshape(NZ, 2, 2, 8, 256).astype(
                jnp.bfloat16
            )

            def send_back(i):
                spot = place * 2 + (core if i % 2 == 0 else 1 - core)
                to = planes[i // 2] * NE + spot
                pltpu.make_async_remote_copy(
                    src_ref=result.at[half, planes[i // 2], spot],
                    dst_ref=out_ref.at[:, half, :, columns(me)],
                    send_sem=b_send,
                    recv_sem=b_recv,
                    device_id={"lev": to},
                    device_id_type=MESH,
                ).start()

            for i in (*range(2, 2 * NZ), 1):
                send_back(i)

            @pl.when(r != NX - 1)
            def _():
                send_back(0)

            @pl.when(r == NX - 1)
            def _():
                pltpu.make_async_copy(
                    result.at[half, z, e], out_ref.at[:, half, :, columns(me)], b_recv
                ).start()
            return carry

        lax.fori_loop(0, NX, one_round, 0)

    def step(k, carry):
        @pl.when(k < ROUNDS)
        def _():
            half = lax.div(k, NX)
            g = group(lax.rem(k, NX))
            arrived = field.at[half, :, pl.ds(g * 2, 2), :, :, pl.ds(TS, 2 * TS)]
            pltpu.make_async_copy(arrived, arrived, x_recv.at[half, g]).wait()

            @pl.when(e != 0)
            def _():
                edge(half, g, 0).start()

            @pl.when(e != NE - 1)
            def _():
                edge(half, g, 1).start()

        @pl.when(k < ROUNDS - WINDOW)
        def _():
            send_round(k + WINDOW)

        @pl.when(k == LAG_EDGE)
        def _():
            for copy in matrices:
                copy.wait()

        @pl.when((k >= LAG_EDGE) & (k < ROUNDS + LAG_EDGE))
        def _():
            now = k - LAG_EDGE
            half = lax.div(now, NX)
            g = group(lax.rem(now + 1, NX))
            edge(half, g, 0).wait_recv()
            edge(half, g, 1).wait_recv()
            rows = field[half, :, pl.ds(g * 2, 2)].reshape(256, 4 * TS)
            for side in range(2):
                part_out[side, half, g] = lax.dot_general(
                    rows, weights_in[side], nt, preferred_element_type=jnp.float32
                ).astype(jnp.bfloat16)
                part(half, g, side).start()
            own[half, g] = lax.dot_general(
                rows, weights[1], nt, preferred_element_type=jnp.float32
            )

        @pl.when(k >= LAG_SUM)
        def _():
            now = k - LAG_SUM
            half = lax.div(now, NX)
            g = group(lax.rem(now + 1, NX))
            part(half, g, 0).wait()
            part(half, g, 1).wait()
            total = (
                own[half, g]
                + part_in[0, half, g].astype(jnp.float32)
                + part_in[1, half, g].astype(jnp.float32)
            )
            mixed[half, :, g] = total.reshape(NZ, 32, 256).astype(jnp.bfloat16)

            @pl.when(lax.rem(now, NX) == NX - 1)
            def _():
                answer(half)

        return carry

    lax.fori_loop(0, ROUNDS + LAG_SUM, step, 0)

    for k in range(ROUNDS):
        if k % NX == 0:
            for rows in ((pl.ds(0, NZ - 1), pl.ds(0, 2)), (NZ - 1, pl.ds(0, 1))):
                block = field.at[(0, *rows, slice(None), slice(None), pl.ds(TS, 2 * TS))]
                pltpu.make_async_copy(block, block, x_send.at[k]).wait()
        else:
            block = field.at[0, :, pl.ds(0, 2), :, :, pl.ds(TS, 2 * TS)]
            pltpu.make_async_copy(block, block, x_send.at[k]).wait()
    for half in range(2):
        for side in range(2):
            block = field.at[half, pl.ds(0, NZ - 1), 0, :, :, pl.ds(0, TS)]
            pltpu.make_async_copy(block, block, t_send.at[half, side]).wait()

            @pl.when(e != ENDS[side])
            def _():
                block = field.at[half, 0, 0, :, :, pl.ds(0, TS)]
                pltpu.make_async_copy(block, block, t_send.at[half, side]).wait()

            @pl.when(e != (0 if side == 0 else NE - 1))
            def _():
                for g in range(NX):
                    edge(half, g, side).wait_send()

    block = out_ref.at[:, :, :, pl.ds(0, (NL - 1) * 256)]
    pltpu.make_async_copy(block, block, b_send).wait()
    pltpu.make_async_copy(out_ref, out_ref, b_recv).wait()


def body(probe_field, vertical_corr, kernel_tiles, column_tile, tile_counts):
    bf16 = jnp.bfloat16
    dma = pltpu.SemaphoreType.DMA
    any_space = pl.BlockSpec(memory_space=pl.ANY)
    operands = [
        probe_field.reshape(2, 2, 8, NL * 256),
        vertical_corr,
        kernel_tiles.reshape(2, 9, TS, TS),
        column_tile.reshape(2, 9),
        tile_counts,
    ]
    operands = [pltpu.with_memory_space_constraint(a, pltpu.HBM) for a in operands]
    out = pl.pallas_call(
        kernel,
        out_shape=jax.ShapeDtypeStruct((2, 2, 8, NL * 256), bf16),
        in_specs=[any_space] * 5,
        out_specs=any_space,
        scratch_shapes=[
            pltpu.VMEM((2, NZ, NE, 2, 8, 4 * TS), bf16),
            pltpu.VMEM((3, 256, 512), bf16),
            pltpu.VMEM((2, 256, 512), bf16),
            pltpu.VMEM((NZ, NX, 32, 1024), bf16),
            pltpu.VMEM((2, 9, TS, TS), bf16),
            pltpu.VMEM((TS, TS), bf16),
            pltpu.SMEM((2, 9), jnp.int32),
            pltpu.SMEM((1, 2), jnp.int32),
            pltpu.VMEM((2, NX, 256, 256), jnp.float32),
            pltpu.VMEM((2, 2, NX, 256, 256), bf16),
            pltpu.VMEM((2, 2, NX, 256, 256), bf16),
            pltpu.VMEM((2, NZ, NX, 32, 256), bf16),
            pltpu.VMEM((2, NZ, NE, 2, 8, 256), bf16),
            dma((4,)),
            dma((ROUNDS,)),
            dma((2, NX)),
            dma((2, 2)),
            dma((2, 2)),
            dma((2, 2)),
            dma((2, NX, 2)),
            dma((2, NX, 2)),
            dma((2, NX, 2)),
            dma((2, NX, 2)),
            dma,
            dma,
        ],
        compiler_params=pltpu.CompilerParams(
            collective_id=0, has_side_effects=True, vmem_limit_bytes=40 * 1024 * 1024
        ),
    )(*operands)
    return out.reshape(2, 16, 1, NL * 256)


def solution(mesh):
    placed = (
        P("lev", None, "col", None),
        P(),
        P("col", "lev", None, None, None),
        P("col", "lev", None),
        P("col", "lev"),
    )
    return jax.shard_map(
        body, mesh=mesh, in_specs=placed, out_specs=P("lev", None, "col", None), check_vma=False
    )
```
